256 devices in a mesh: row: 32 (over z, x_lo, core), col: 8 (over x_hi, y).
Axes of the slice: x: 4 (x_hi: 2, x_lo: 2; x = x_hi * 2 + x_lo), y: 4, z: 8, core: 2. Of those that a mesh axis runs over, the one named last changes fastest.
Arguments:
- polar_rays: bfloat16 [256, 360, 256], P(('row', 'col')), may hold values from -6 to 6
- first_line: int32 [256, 32, 8], P('row', None, 'col'), may hold values from 0 to 359
- second_line: int32 [256, 32, 8], P('row', None, 'col'), may hold values from 0 to 179
- start_frame: float32 [3, 3, 256], P(None, None, ('row', 'col')), may hold values from -6 to 6
Outputs:
- line_scores: float32 [256, 32, 8], P('row', None, 'col')
- estimates: float32 [3, 3, 256], P(None, None, ('row', 'col'))
The draws below stay inside these ranges and needn't reach their ends.
All inputs are finite; a program needn't handle non-finite values. Where the reference program divides by a largest or mean magnitude, that divisor is 1e-20 or more.
Results may differ from the reference program's by a relative error of at most 0.0003.
Values may be sent and summed in bfloat16 or wider, within the bound.
A program may use at most 64 MiB of HBM per device.

```python
import math
import jax
import jax.numpy as jnp
from jax import lax

L = 360
R = 128
ITERS = 3
N = 256
IMG_R = 8
N_ROW = 32


def set_ends(drawn, key, least, high):
    place = [jax.random.randint(jax.random.fold_in(key, axis), (), 0, length) for axis, length in enumerate(drawn.shape)]
    longest = drawn.shape.index(max(drawn.shape))
    neighbour = place[:longest] + [(place[longest] + 1) % drawn.shape[longest]] + place[longest + 1:]
    return drawn.at[tuple(place)].set(least).at[tuple(neighbour)].set(high)


def levels(stream_key, dims, pieces, smallest, largest):
    loudness = 1.0
    for axis_at, blocks in pieces:
        steps = jax.random.uniform(jax.random.fold_in(jax.random.fold_in(stream_key, 6), axis_at), (blocks,), jnp.float32, smallest / len(pieces), largest / len(pieces))
        loudness = loudness * jnp.repeat(jnp.exp(steps), dims[axis_at] // blocks).reshape((-1,) + (1,) * (len(dims) - 1 - axis_at))
    return loudness


def noise(key, dims, scale, limit, cuts=(), held_as=jnp.bfloat16):
    drawn = jax.random.normal(key, dims, jnp.float32) * scale
    if len(cuts) > 0:
        drawn = levels(key, dims, cuts, -0.22, 0.18) * drawn
    return jnp.clip(drawn, min=-limit, max=limit).astype(held_as)


def setup_inputs(seed: int = 0) -> dict:
    seeds = jax.random.split(jax.random.key(seed), 5)
    return {
        "polar_rays": noise(seeds[0], (N, L, 2 * R), 1.0, 6.0, ((0, 256),)),
        "first_line": set_ends(jax.random.randint(seeds[1], (N, N_ROW, IMG_R), 0, L), jax.random.fold_in(seeds[1], 1), 0, L - 1).astype(jnp.int32),
        "second_line": set_ends(jax.random.randint(seeds[2], (N, N_ROW, IMG_R), 0, L // 2), jax.random.fold_in(seeds[2], 1), 0, (L // 2) - 1).astype(jnp.int32),
        "start_frame": noise(seeds[3], (3, 3, N), 1.0, 6.0, ((2, 256),), jnp.float32),
    }


def unit_vectors(angle):
    phases = angle.astype(jnp.float32) * (2.0 * math.pi / L)
    return jnp.stack([jnp.cos(phases), jnp.sin(phases), jnp.ones_like(phases)])

def lower_solve(factor, values):
    first_row = values[0] / factor[0, 0]
    second_row = (values[1] - factor[1, 0] * first_row) / factor[1, 1]
    third_row = (values[2] - factor[2, 0] * first_row - factor[2, 1] * second_row) / factor[2, 2]
    return jnp.stack([first_row, second_row, third_row])

def reference(polar_rays, first_line, second_line, start_frame):
    image_count = polar_rays.shape[0]
    first_table = first_line.reshape(image_count, image_count)
    second_table = second_line.reshape(image_count, image_count)
    real_rays = polar_rays.astype(jnp.float32)
    half_rays = real_rays[:, :L // 2]
    exact = lax.Precision.HIGHEST

    def score_row(inputs):
        own_rays, first_row, second_row = inputs
        corr = jnp.einsum('ar,jbr->jab', own_rays, half_rays, precision=exact)
        center = corr - lax.optimization_barrier(jnp.mean(corr, axis=(1, 2), keepdims=True))
        spread = lax.optimization_barrier(jnp.mean(jnp.abs(center), axis=(1, 2)))
        picked = jnp.take_along_axis(center, first_row[:, None, None], axis=1)[:, 0, :]
        picked = jnp.take_along_axis(picked, second_row[:, None], axis=1)[:, 0]
        return picked / (spread + 1e-05)
    scores = lax.map(score_row, (real_rays, first_table, second_table))
    first_units = unit_vectors(first_table)
    second_weighted = scores[None] * unit_vectors(second_table)
    frames = start_frame
    for turn_index in range(ITERS):
        mixed = jnp.einsum('qij,kqj->kij', second_weighted, frames, precision=exact)
        applied = jnp.einsum('pij,kij->kpi', first_units, mixed, precision=exact)
        gram_matrix = jnp.einsum('kpi,lpi->kl', applied, applied, precision=exact)
        factor = jnp.linalg.cholesky(gram_matrix)
        frames = lower_solve(factor, applied)
    return (scores.reshape(first_line.shape), jnp.sqrt(jnp.float32(image_count)) * frames)
```

```python
import functools
import math

import jax
import jax.numpy as jnp
from jax import lax
from jax.experimental import pallas as pl
from jax.experimental.pallas import tpu as pltpu
from jax.sharding import PartitionSpec as P

L = 360
HALF = 180
ITERS = 3
N = 256
PITCH = 192
SENT = 184
CUT = 176
GROUP = 4 * PITCH
TILE = 256
F32 = jnp.float32
BF16 = jnp.bfloat16
MESH = pl.DeviceIdType.MESH
HIGHEST = lax.Precision.HIGHEST


def iota(shape, dim):
    return lax.broadcasted_iota(jnp.int32, shape, dim)


def split3(x):
    hi = x.astype(BF16)
    rest = x - hi.astype(F32)
    mid = rest.astype(BF16)
    low = (rest - mid.astype(F32)).astype(BF16)
    return hi, mid, low


def permute(x, perm):
    parts = jnp.concatenate(split3(x), axis=0)
    out = jnp.dot(parts, perm, preferred_element_type=F32)
    return out[0:32] + out[32:64] + out[64:96]


def kernel(
    rays, first_ref, second_ref, second_sm, frame_ref,
    scores_ref, est_ref,
    img, grp, sel, sum_i, sum_j, first_t, acc_s, acc_m, acc_p,
    pkt, pk, own_sc, sg, yz, perm_ref, trig, hmat,
    send_sem, img_sem, grp_sem, loc_sem, many_send, many_recv,
):
    row = lax.axis_index("row")
    col = lax.axis_index("col")
    z, t, co = row // 4, (row // 2) % 2, row % 2
    xh, y = col // 4, col % 4
    rl = row % 4
    pid = rl * 8 + col
    rr = (rl, (1 - t) * 2 + co, t * 2 + 1 - co, (1 - t) * 2 + 1 - co)

    core_peer = (z * 4 + t * 2 + 1 - co, col)
    xlo_peer = (z * 4 + (1 - t) * 2 + co, col)
    zp = (((z + 1) % 8) * 4 + rl, col)
    zm = (((z + 7) % 8) * 4 + rl, col)
    xhi_peer = (row, (1 - xh) * 4 + y)
    yp = (row, xh * 4 + (y + 1) % 4)
    ym = (row, xh * 4 + (y + 3) % 4)

    own_img = pltpu.make_async_copy(rays.at[0], img.at[0], loc_sem.at[0])
    own_img.start()

    def plane_peer(d):
        peer = (pid + d) % 32
        return (z * 4 + peer // 8, peer % 8)

    def z_peer(d):
        return (((z + d) % 8) * 4 + rl, col)

    barrier = pltpu.get_barrier_semaphore()

    def greet_plane(d, _):
        pl.semaphore_signal(barrier, inc=1, device_id=plane_peer(d), device_id_type=MESH)
        return 0

    def greet_z(d, _):
        pl.semaphore_signal(barrier, inc=1, device_id=z_peer(d), device_id_type=MESH)
        return 0

    lax.fori_loop(1, 32, greet_plane, 0)
    lax.fori_loop(1, 8, greet_z, 0)
    own_img.wait()

    def half(slot, block):
        return grp.at[slot, pl.ds(pl.multiple_of(block * PITCH, PITCH), SENT), :]

    own_half = pltpu.make_async_copy(img.at[0, pl.ds(0, SENT), :], half(0, rl), loc_sem.at[1])
    own_half.start()

    lane = iota((8, 128), 1)
    pkt[...] = jnp.zeros((2, 8, 128), F32)
    pkt[0, 0:8, 0:32] = (first_ref[...] + 512 * second_ref[...]).astype(F32)
    pkt[1, 0:3, 0:3] = frame_ref[...]
    packed = pkt[0]
    frame = pkt[1]
    for q in range(3):
        packed = packed + jnp.where(lane == 32 + q * 32 + pid, frame[:, q : q + 1], 0.0)
    pkt[0] = packed
    pk[pid] = packed
    own_half.wait()
    pl.semaphore_wait(barrier, 38)

    pending = []

    def send(src, dst, sem, dev):
        copy = pltpu.make_async_remote_copy(
            src_ref=src, dst_ref=dst, send_sem=send_sem.at[len(pending)], recv_sem=sem,
            device_id=dev, device_id_type=MESH,
        )
        copy.start()
        pending.append(copy)

    def landed(dst, sem):
        pltpu.make_async_remote_copy(
            src_ref=dst, dst_ref=dst, send_sem=send_sem.at[0], recv_sem=sem,
            device_id=core_peer, device_id_type=MESH,
        ).wait_recv()

    def send_half(slot, k, to_slot, to_k, dev):
        send(half(slot, rr[k]), half(to_slot, rr[k]), grp_sem.at[to_slot * 4 + to_k], dev)

    def half_landed(slot, k):
        landed(half(slot, rr[k]), grp_sem.at[slot * 4 + k])

    def whole(slot):
        return img.at[slot]

    def top(slot):
        return img.at[slot, pl.ds(0, CUT), :]

    def bottom(slot):
        return img.at[slot, pl.ds(CUT, L - CUT), :]

    send_half(0, 0, 0, 1, xlo_peer)
    send_half(0, 0, 2, 0, zp)
    send_half(0, 0, 1, 0, zm)
    send_half(0, 0, 0, 2, core_peer)
    send(whole(0), whole(4), img_sem.at[4], xhi_peer)
    send(whole(0), whole(2), img_sem.at[2], yp)
    send(whole(0), whole(1), img_sem.at[1], ym)

    def send_all(src, dst, count, peer_of, n):
        def one(d, _):
            pltpu.make_async_remote_copy(
                src_ref=src, dst_ref=dst, send_sem=many_send.at[n], recv_sem=many_recv.at[n],
                device_id=peer_of(d), device_id_type=MESH,
            ).start()
            return 0

        lax.fori_loop(1, count, one, 0)

    def all_landed(buf, count, n):
        part = buf.at[pl.ds(0, count - 1)]
        pltpu.make_async_remote_copy(
            src_ref=part, dst_ref=part, send_sem=many_send.at[n], recv_sem=many_recv.at[n],
            device_id=core_peer, device_id_type=MESH,
        ).wait()

    send_all(pkt.at[0], pk.at[pid], 32, plane_peer, 0)

    pr, pc = iota((N, N), 0), iota((N, N), 1)
    perm = jnp.where((pr // 32 == pc % 8) & (pr % 32 == pc // 8), 1.0, 0.0).astype(BF16)
    perm_ref[...] = perm
    padded = jnp.where(lane < 32, packed, 0.0).astype(jnp.int32)
    first_t[...] = jnp.transpose((padded % 512).astype(F32))
    acc_s[...] = jnp.zeros((8, 128), F32)
    acc_m[...] = jnp.zeros((8, 128), F32)
    acc_p[...] = jnp.zeros((8, 128), F32)

    def image_of(slot):
        k = slot % 4
        dy = k + (k // 2) * (5 - 2 * k)
        return ((xh + slot // 4) % 2) * 4 + (y + dy) % 4

    def plane_of(slot):
        return (z + ((slot + 1) // 2) * (2 * (slot % 2) - 1) + 8) % 8

    lanes_t = iota((32, 128), 1)

    def prep_image(slot, _):
        which = image_of(slot)
        ray = jnp.sum(jnp.where(lanes_t == which, jnp.pad(first_t[0:32, :], ((0, 0), (0, 120))), 0.0), axis=1, keepdims=True)
        data = img[slot]
        hot = jnp.where(iota((32, L), 1).astype(F32) == ray, 1.0, 0.0).astype(BF16)
        sel[slot] = jnp.dot(hot, data, preferred_element_type=F32).astype(BF16)
        total = jnp.sum(data.astype(F32).reshape(L // 8, 8, 256), axis=0)
        sum_i[slot] = jnp.broadcast_to(jnp.sum(total, axis=0, keepdims=True), (8, 256))
        return 0

    def prep_group(slot, _):
        for k in range(4):
            data = grp[slot, k * PITCH : k * PITCH + HALF, :].astype(F32)
            sum_j[slot, k : k + 1, :] = jnp.sum(data, axis=0, keepdims=True)
        return 0

    cols = iota((1, GROUP), 1)
    seg = cols // PITCH
    inside = cols % PITCH < HALF

    def unit(i, s):
        which, plane = image_of(i), plane_of(s)
        means = jnp.sum(sum_j[s] * sum_i[i], axis=1, keepdims=True) * (1.0 / (L * HALF))
        m_row = jnp.zeros((1, GROUP), F32)
        target = jnp.zeros((1, GROUP), jnp.int32)
        for k in range(4):
            m_row = jnp.where(seg == k, means[k : k + 1, :], m_row)
            target = jnp.where(seg == k, k * PITCH + second_sm[which, plane * 4 + k], target)
        lhs = jnp.concatenate([sel[i, pl.ds(pl.multiple_of((plane // 4) * 16, 16), 16), :], img[i]], axis=0)
        hit_row = (plane % 4) * 4 + seg
        found = []
        for c in range(0, GROUP, TILE):
            d = lax.dot_general(lhs, grp[s, c : c + TILE, :], (((1,), (1,)), ((), ())), preferred_element_type=F32)
            dev = jnp.sum(jnp.abs(d[16:] - m_row[:, c : c + TILE]).reshape(L // 8, 8, TILE), axis=0)
            hit = (cols[:, c : c + TILE] == target[:, c : c + TILE]) & (iota((16, TILE), 0) == hit_row[:, c : c + TILE])
            pick = jnp.where(hit, d[:16], 0.0)
            found.append(jnp.concatenate([dev, pick[0:8] + pick[8:16]], axis=0))
        both = jnp.concatenate(found, axis=1)
        here_i = iota((8, 128), 0) == which
        res_s, res_m, res_p = acc_s[...], acc_m[...], acc_p[...]
        for k in range(4):
            part = jnp.sum(jnp.where((seg == k) & inside, both, 0.0), axis=1, keepdims=True)
            here = here_i & (lane == plane * 4 + k)
            res_s = jnp.where(here, jnp.sum(part[0:8], axis=0, keepdims=True), res_s)
            res_p = jnp.where(here, jnp.sum(part[8:16], axis=0, keepdims=True), res_p)
            res_m = jnp.where(here, means[k : k + 1, :], res_m)
        acc_s[...], acc_m[...], acc_p[...] = res_s, res_m, res_p

    def block(i0, i1, s0, s1):
        def body(s, _):
            for i in range(i0, i1):
                unit(i, s)
            return 0

        lax.fori_loop(s0, s1, body, 0)

    half_landed(0, 1)
    send_half(0, 1, 2, 1, zp)
    send_half(0, 1, 1, 1, zm)
    send_half(0, 1, 0, 3, core_peer)
    lax.fori_loop(0, 1, prep_image, 0)

    def hop(to_slot, from_p, from_m, k):
        half_landed(from_p, k)
        if to_slot is not None:
            send_half(from_p, k, to_slot, k, zm)
        send_half(from_p, k, from_p, k + 2, core_peer)
        half_landed(from_m, k)
        if to_slot is not None:
            send_half(from_m, k, to_slot + 1, k, zp)
        send_half(from_m, k, from_m, k + 2, core_peer)

    hop(3, 1, 2, 0)
    half_landed(0, 2)
    half_landed(0, 3)
    landed(whole(1), img_sem.at[1])
    send(bottom(1), bottom(3), img_sem.at[3], ym)
    landed(whole(2), img_sem.at[2])
    send(top(2), top(3), img_sem.at[8], yp)
    hop(3, 1, 2, 1)
    lax.fori_loop(1, 3, prep_image, 0)
    landed(whole(4), img_sem.at[4])
    send(whole(4), whole(6), img_sem.at[6], yp)
    send(whole(4), whole(5), img_sem.at[5], ym)
    for slot in (1, 2):
        for k in (2, 3):
            half_landed(slot, k)
    lax.fori_loop(0, 3, prep_group, 0)
    block(0, 3, 0, 3)

    hop(5, 3, 4, 0)
    landed(bottom(3), img_sem.at[3])
    landed(top(3), img_sem.at[8])
    lax.fori_loop(3, 5, prep_image, 0)
    block(3, 5, 0, 3)
    hop(5, 3, 4, 1)
    for slot in (3, 4):
        for k in (2, 3):
            half_landed(slot, k)
    lax.fori_loop(3, 5, prep_group, 0)
    landed(whole(5), img_sem.at[5])
    send(bottom(5), bottom(7), img_sem.at[7], ym)
    landed(whole(6), img_sem.at[6])
    send(top(6), top(7), img_sem.at[9], yp)
    block(0, 5, 3, 5)

    half_landed(5, 0)
    send_half(5, 0, 5, 2, core_peer)
    half_landed(6, 0)
    send_half(6, 0, 7, 0, zp)
    send_half(6, 0, 6, 2, core_peer)
    half_landed(5, 1)
    send_half(5, 1, 7, 1, zm)
    send_half(5, 1, 5, 3, core_peer)
    half_landed(6, 1)
    send_half(6, 1, 6, 3, core_peer)
    landed(bottom(7), img_sem.at[7])
    landed(top(7), img_sem.at[9])
    lax.fori_loop(5, 8, prep_image, 0)
    block(5, 8, 0, 5)
    for slot in (5, 6):
        for k in (2, 3):
            half_landed(slot, k)
    half_landed(7, 0)
    send_half(7, 0, 7, 2, core_peer)
    half_landed(7, 1)
    send_half(7, 1, 7, 3, core_peer)

    all_landed(pk, 32, 0)

    def plane_tables(buf, shift):
        rows = []
        for r in range(4):
            tiles = []
            for h in range(2):
                tile = jnp.zeros((8, 128), F32)
                for c in range(4):
                    part = buf[r * 8 + h * 4 + c]
                    if shift:
                        part = jnp.where(lane < 32, part, 0.0)
                        part = pltpu.roll(part, 32 * c, 1) if c else part
                    tile = tile + part
                tiles.append(tile)
            rows.append(jnp.concatenate(tiles, axis=1))
        return jnp.concatenate(rows, axis=0)

    table = permute(plane_tables(pk, True), perm_ref[...]).astype(jnp.int32)
    angle_a = (table % 512).astype(F32) * (2.0 * math.pi / L)
    angle_b = (table // 512).astype(F32) * (2.0 * math.pi / L)
    one = jnp.ones((32, N), F32)
    unit_a = (jnp.cos(angle_a), jnp.sin(angle_a), one)
    unit_b = (jnp.cos(angle_b), jnp.sin(angle_b), one)
    for p in range(3):
        for q in range(3):
            trig[p * 32 : p * 32 + 32, q * N : q * N + N] = unit_a[p] * unit_b[q]
    frames = pk[0]
    for d in range(1, 32):
        frames = frames + pk[d]
    frames = jnp.where(lane < 96, pltpu.roll(frames, 96, 1), 0.0)
    yz[0, z] = frames
    send_all(yz.at[0, z], yz.at[0, z], 8, z_peer, 1)

    lax.fori_loop(5, 7, prep_group, 0)
    block(0, 8, 5, 7)
    half_landed(7, 2)
    half_landed(7, 3)
    lax.fori_loop(7, 8, prep_group, 0)
    block(0, 8, 7, 8)

    spread = acc_s[...] * (1.0 / (L * HALF))
    scores = (acc_p[...] - acc_m[...]) / (spread + 1e-05)
    scores = jnp.where(lane < 32, scores, 0.0)
    scores_ref[...] = scores[:, 0:32]
    wide = scores + pltpu.roll(scores, 32, 1) + pltpu.roll(scores, 64, 1) + pltpu.roll(scores, 96, 1)
    wide = jnp.where(lane // 32 == col % 4, wide, 0.0)
    own_sc[...] = wide
    sg[pid] = wide
    send_all(own_sc, sg.at[pid], 32, plane_peer, 2)
    all_landed(yz.at[0], 8, 1)
    all_landed(sg, 32, 2)
    table_s = permute(plane_tables(sg, False), perm_ref[...])
    hmat[96:128, :] = jnp.zeros((32, 3 * N), F32)
    for p in range(3):
        for q in range(3):
            at = (slice(p * 32, p * 32 + 32), slice(q * N, q * N + N))
            hmat[at] = trig[at] * table_s

    def gathered(n):
        tiles = []
        for q in range(3):
            for h in range(2):
                tile = jnp.zeros((8, 128), F32)
                for k in range(4):
                    part = yz[n, h * 4 + k]
                    shift = ((k - q) * 32) % 128
                    part = pltpu.roll(part, shift, 1) if shift else part
                    tile = jnp.where(lane // 32 == k, part, tile)
                tiles.append(tile)
        return jnp.concatenate(tiles, axis=1)

    def orthonormal(v):
        g = [jnp.sum(v * v[k : k + 1, :], axis=1, keepdims=True) for k in range(3)]
        f00 = jnp.sqrt(g[0][0:1])
        f10 = g[0][1:2] / f00
        f20 = g[0][2:3] / f00
        f11 = jnp.sqrt(g[1][1:2] - f10 * f10)
        f21 = (g[1][2:3] - f20 * f10) / f11
        f22 = jnp.sqrt(g[2][2:3] - f20 * f20 - f21 * f21)
        v0 = v[0:1] / f00
        v1 = (v[1:2] - f10 * v0) / f11
        v2 = (v[2:3] - f20 * v0 - f21 * v1) / f22
        return jnp.concatenate([v0, v1, v2, jnp.zeros((5, 3 * N), F32)], axis=0)

    v = gathered(0)
    for n in range(1, ITERS + 1):
        out = lax.dot_general(v, hmat[...], (((1,), (1,)), ((), ())), precision=HIGHEST, preferred_element_type=F32)
        yz[n, z] = out
        send_all(yz.at[n, z], yz.at[n, z], 8, z_peer, n + 2)
        all_landed(yz.at[n], 8, n + 2)
        v = orthonormal(gathered(n))

    place = iota((8, 3 * N), 1)
    mine = z * 32 + pid
    for p in range(3):
        value = jnp.sum(jnp.where(place == p * N + mine, v, 0.0), axis=1, keepdims=True)
        est_ref[:, 0, p : p + 1] = math.sqrt(N) * value[0:3]

    for copy in pending:
        copy.wait_send()


def per_device(polar_rays, first_line, second_line, start_frame):
    first = first_line.reshape(8, 32)
    second = second_line.reshape(8, 32)
    vm = pl.BlockSpec(memory_space=pltpu.VMEM)
    scores, est = pl.pallas_call(
        kernel,
        out_shape=(jax.ShapeDtypeStruct((8, 32), F32), jax.ShapeDtypeStruct((3, 1, 3), F32)),
        in_specs=[
            pl.BlockSpec(memory_space=pl.ANY), vm, vm, pl.BlockSpec(memory_space=pltpu.SMEM), vm,
        ],
        out_specs=(vm, vm),
        scratch_shapes=[
            pltpu.VMEM((8, L, 256), BF16),
            pltpu.VMEM((8, GROUP, 256), BF16),
            pltpu.VMEM((8, 32, 256), BF16),
            pltpu.VMEM((8, 8, 256), F32),
            pltpu.VMEM((8, 8, 256), F32),
            pltpu.VMEM((128, 8), F32),
            pltpu.VMEM((8, 128), F32),
            pltpu.VMEM((8, 128), F32),
            pltpu.VMEM((8, 128), F32),
            pltpu.VMEM((2, 8, 128), F32),
            pltpu.VMEM((32, 8, 128), F32),
            pltpu.VMEM((8, 128), F32),
            pltpu.VMEM((32, 8, 128), F32),
            pltpu.VMEM((ITERS + 1, 8, 8, 128), F32),
            pltpu.VMEM((N, N), BF16),
            pltpu.VMEM((96, 3 * N), F32),
            pltpu.VMEM((128, 3 * N), F32),
            pltpu.SemaphoreType.DMA((48,)),
            pltpu.SemaphoreType.DMA((10,)),
            pltpu.SemaphoreType.DMA((32,)),
            pltpu.SemaphoreType.DMA((2,)),
            pltpu.SemaphoreType.DMA((6,)),
            pltpu.SemaphoreType.DMA((6,)),
        ],
        compiler_params=pltpu.CompilerParams(
            collective_id=0, has_side_effects=True, vmem_limit_bytes=48 << 20
        ),
    )(polar_rays, first, second, second, start_frame.reshape(3, 3))
    return scores.reshape(first_line.shape), est.transpose(0, 2, 1)


def solution(mesh):
    placed = (
        P(("row", "col"), None, None),
        P("row", None, "col"),
        P("row", None, "col"),
        P(None, None, ("row", "col")),
    )
    return jax.shard_map(
        per_device,
        mesh=mesh,
        in_specs=placed,
        out_specs=(P("row", None, "col"), P(None, None, ("row", "col"))),
        check_vma=False,
    )
```
